32 devices in a mesh: sec: 4 (over x, core), key: 8 (over z, y).
Axes of the slice: x: 2, y: 2, z: 4, core: 2. Of those that a mesh axis runs over, the one named last changes fastest.
Arguments:
- query: bfloat16 [4096, 16, 128], P(('sec', 'key')), may hold values from -64 to 64
- key: bfloat16 [4096, 4, 128], P(('sec', 'key')), may hold values from -5 to 5
- value: bfloat16 [4096, 4, 128], P(('sec', 'key')), may hold values from -5 to 5
- raw_directions: bfloat16 [4096, 4, 128], P(('sec', 'key')), may hold values from -5 to 5
- beta_raw_logits: float32 [4096, 4], P(('sec', 'key')), may hold values from -7 to 7
Outputs:
- attended: bfloat16 [4096, 16, 128], P(('sec', 'key'))
The draws below stay inside these ranges and needn't reach their ends.
All inputs are finite; a program needn't handle non-finite values.
Results may differ from the reference program's by a relative error of at most 0.0055.
Values sent between devices are 32-bit elements; how exact they have to be, the bound alone decides.
No kernel may reach another device: no remote copies, remote signals or barrier semaphores. Data moves between devices by JAX's collectives and lax.ppermute only.
A program may use at most 64 MiB of HBM per device.

```python
import jax
import jax.numpy as jnp
from jax import lax

HEAD_WIDTH = 128
QUERY_HEADS = 16
KEY_VALUE_HEADS = 4
TOKENS_PER_PART = 128
SEQUENCE_TOKENS = 4096


def head_ordering(key):
    ordering_random_key = jax.random.fold_in(jax.random.fold_in(key, 23), 0)
    return jax.random.permutation(ordering_random_key, KEY_VALUE_HEADS)


def draw_query(key, part):
    base_key = jax.random.fold_in(jax.random.fold_in(key, 11), 0)
    base = jnp.clip(jax.random.normal(base_key, (SEQUENCE_TOKENS, QUERY_HEADS, HEAD_WIDTH), jnp.float32), -4.0, 4.0)
    return base.astype(jnp.bfloat16)


def draw_raw_directions(key, part):
    token_ordering = head_ordering(key)
    quick_heads = token_ordering >= KEY_VALUE_HEADS // 2
    basis_key, pick_key, size_key, sign_key, noise_key, drawn_key = jax.random.split(jax.random.fold_in(key, 37), 6)
    basis_vectors = jnp.clip(jax.random.normal(basis_key, (KEY_VALUE_HEADS, 4, HEAD_WIDTH), jnp.float32), -3.0, 3.0)
    picked_rows = jax.random.randint(pick_key, (SEQUENCE_TOKENS, KEY_VALUE_HEADS), 0, 4)
    head_numbers = jnp.arange(KEY_VALUE_HEADS)[None, :]
    chosen_vectors = basis_vectors[head_numbers, picked_rows]
    token_signs = jnp.where(jax.random.bernoulli(sign_key, 0.5, (SEQUENCE_TOKENS, KEY_VALUE_HEADS, 1)), 1.0, -1.0)
    token_sizes = token_signs * jax.random.uniform(size_key, (SEQUENCE_TOKENS, KEY_VALUE_HEADS, 1), jnp.float32, 0.5, 1.5)
    noise_rows = jnp.clip(jax.random.normal(noise_key, (SEQUENCE_TOKENS, KEY_VALUE_HEADS, HEAD_WIDTH), jnp.float32), -4.0, 4.0)
    confined_rows = token_sizes * chosen_vectors + 0.1 * noise_rows
    drawn_rows = jnp.clip(jax.random.normal(drawn_key, (SEQUENCE_TOKENS, KEY_VALUE_HEADS, HEAD_WIDTH), jnp.float32), -5.0, 5.0)
    return jnp.where(quick_heads[None, :, None], confined_rows, drawn_rows).astype(jnp.bfloat16)


def draw_beta_raw_logits(key, part):
    signs_random_key = jax.random.fold_in(jax.random.fold_in(key, 23), 1)
    sizes_random_key = jax.random.fold_in(jax.random.fold_in(key, 23), 2)
    quick_random_key = jax.random.fold_in(jax.random.fold_in(key, 23), 3)
    token_ordering = head_ordering(key)
    slower_path = token_ordering < KEY_VALUE_HEADS // 2
    random_signs = jnp.where(jax.random.bernoulli(signs_random_key, 0.5, (SEQUENCE_TOKENS, KEY_VALUE_HEADS)), 1.0, -1.0)
    slower_value_rows = random_signs * jax.random.uniform(sizes_random_key, (SEQUENCE_TOKENS, KEY_VALUE_HEADS), jnp.float32, 4.0, 7.0)
    quick_value_rows = jax.random.uniform(quick_random_key, (SEQUENCE_TOKENS, KEY_VALUE_HEADS), jnp.float32, -2.0, 2.0)
    return jnp.where(slower_path[None, :], slower_value_rows, quick_value_rows).astype(jnp.float32)


def block_scale(own_key, extent, cuts, least, top_value):
    loudness = 1.0
    for axis_at, parts in cuts:
        draws = jax.random.uniform(jax.random.fold_in(jax.random.fold_in(own_key, 6), axis_at), (parts,), jnp.float32, least / len(cuts), top_value / len(cuts))
        loudness = loudness * jnp.repeat(jnp.exp(draws), extent[axis_at] // parts).reshape((-1,) + (1,) * (len(extent) - 1 - axis_at))
    return loudness


def normal_values(rng, shape, scale, reach, pieces=(), held_as=jnp.bfloat16):
    factor_of = block_scale(rng, shape, pieces, -0.22, 0.18) if pieces else 1.0
    entries = jax.random.normal(rng, shape, jnp.float32) * scale * factor_of
    return jnp.minimum(jnp.maximum(entries, -reach), reach).astype(held_as)


def setup_inputs(seed: int = 0) -> dict:
    keys = jax.random.split(jax.random.key(seed), 6)
    query = draw_query(jax.random.fold_in(keys[5], 71), 0)
    key = normal_values(keys[1], (SEQUENCE_TOKENS, KEY_VALUE_HEADS, HEAD_WIDTH), 1.0, 5.0, ((0, 32),))
    value = normal_values(keys[2], (SEQUENCE_TOKENS, KEY_VALUE_HEADS, HEAD_WIDTH), 1.0, 5.0, ((0, 32),))
    raw_directions = draw_raw_directions(jax.random.fold_in(keys[5], 71), 0)
    beta_raw_logits = draw_beta_raw_logits(jax.random.fold_in(keys[5], 71), 0)
    return dict(query=query, key=key, value=value, raw_directions=raw_directions, beta_raw_logits=beta_raw_logits)


highest = lax.Precision.HIGHEST

def block_terms(query, key, raw_directions, beta_raw_logits):
    length = key.shape[0]
    heads = key.shape[1]
    width = key.shape[2]
    query_group = query.shape[1] // heads
    w_float = raw_directions.astype(jnp.float32)
    w_unit = w_float / jnp.sqrt(lax.optimization_barrier(jnp.sum(w_float * w_float, -1, keepdims=True)) + 1e-06)
    beta = 2.0 * jax.nn.sigmoid(beta_raw_logits)
    w_heads = jnp.transpose(w_unit, (1, 0, 2))
    k_heads = jnp.transpose(key.astype(jnp.float32), (1, 0, 2))
    b_heads = jnp.transpose(beta, (1, 0))[:, :, None]
    positions = jnp.arange(length)
    strict = (positions[:, None] > positions[None, :]).astype(jnp.float32)
    lower = (positions[:, None] >= positions[None, :]).astype(jnp.float32)
    gram = jnp.einsum('hte,hse->hts', w_heads, w_heads, precision=highest) * strict
    system = jnp.eye(length, dtype=jnp.float32) + b_heads * gram
    cross = jnp.einsum('hte,hse->hts', w_heads, k_heads, precision=highest) * strict
    right = jnp.concatenate([b_heads * w_heads, b_heads * cross], axis=2)
    solved = lax.linalg.triangular_solve(system, right, left_side=True, lower=True, unit_diagonal=True)
    y_rows = solved[:, :, :width]
    z_rows = solved[:, :, width:]
    block_map = jnp.eye(width, dtype=jnp.float32) - jnp.einsum('hte,htf->hef', w_heads, y_rows, precision=highest)
    key_end = k_heads - jnp.einsum('hts,hte->hse', z_rows, w_heads, precision=highest)
    q_heads = jnp.transpose(query.astype(jnp.float32).reshape(length, heads, query_group, width), (1, 2, 0, 3))
    q_dot_w = jnp.einsum('hgie,hte->hgit', q_heads, w_heads, precision=highest) * lower
    query_start = q_heads - jnp.einsum('hgit,hte->hgie', q_dot_w, y_rows, precision=highest)
    inner = jnp.einsum('hgie,hje->hgij', q_heads, k_heads, precision=highest)
    inner = inner - jnp.einsum('hgit,htj->hgij', q_dot_w, z_rows, precision=highest)
    query_start = query_start.reshape(heads, query_group * length, width)
    inner = inner.reshape(heads, query_group * length, length) * width ** (-0.5)
    return (query_start, key_end, block_map, inner)

def attend(state, scores, values, valid):
    score_maxima, weighted_totals, exponent_sums = state
    masked = jnp.where(valid, scores, -1e+30)
    new_max = jnp.maximum(score_maxima, lax.optimization_barrier(jnp.max(masked, -1)))
    weights = jnp.where(valid, jnp.exp(masked - new_max[..., None]), 0.0)
    factor = jnp.exp(score_maxima - new_max)
    weighted_totals = weighted_totals * factor + lax.optimization_barrier(jnp.sum(weights, -1))
    rounded = lax.optimization_barrier(weights.astype(jnp.bfloat16)).astype(jnp.float32)
    exponent_sums = exponent_sums * factor[..., None] + jnp.einsum('...ij,...je->...ie', rounded, values.astype(jnp.float32), precision=highest)
    return (new_max, weighted_totals, exponent_sums)

def reference(query, key, value, raw_directions, beta_raw_logits):
    block_list = SEQUENCE_TOKENS // TOKENS_PER_PART
    query_group = QUERY_HEADS // KEY_VALUE_HEADS
    q_blocks = query.reshape(block_list, TOKENS_PER_PART, QUERY_HEADS, HEAD_WIDTH)
    key_block_list = key.reshape(block_list, TOKENS_PER_PART, KEY_VALUE_HEADS, HEAD_WIDTH)
    direction_block_list = raw_directions.reshape(block_list, TOKENS_PER_PART, KEY_VALUE_HEADS, HEAD_WIDTH)
    beta_block_list = beta_raw_logits.reshape(block_list, TOKENS_PER_PART, KEY_VALUE_HEADS)
    query_start, key_end, block_map, inner = jax.vmap(block_terms)(q_blocks, key_block_list, direction_block_list, beta_block_list)
    value_head_rows = jnp.transpose(value.reshape(block_list, TOKENS_PER_PART, KEY_VALUE_HEADS, HEAD_WIDTH), (0, 2, 1, 3))
    positions = jnp.arange(TOKENS_PER_PART)
    causal = jnp.tile(positions[:, None] >= positions[None, :], (query_group, 1))
    score_maxima = jnp.full((block_list, KEY_VALUE_HEADS, query_group * TOKENS_PER_PART), -1e+30, jnp.float32)
    weighted_totals = jnp.zeros((block_list, KEY_VALUE_HEADS, query_group * TOKENS_PER_PART), jnp.float32)
    exponent_sums = jnp.zeros((block_list, KEY_VALUE_HEADS, query_group * TOKENS_PER_PART, HEAD_WIDTH), jnp.float32)
    score_maxima, weighted_totals, exponent_sums = attend((score_maxima, weighted_totals, exponent_sums), inner, value_head_rows, causal)
    block_ids = jnp.arange(block_list)

    def advance(step, carry):
        score_maxima, weighted_totals, exponent_sums, moving = carry
        keys_back = jnp.roll(key_end, step, axis=0)
        values_back = jnp.roll(value_head_rows, step, axis=0)
        maps_back = jnp.roll(block_map, step, axis=0)
        scores = jnp.einsum('nhie,nhje->nhij', moving, keys_back, precision=highest) * HEAD_WIDTH ** (-0.5)
        valid = (block_ids >= step)[:, None, None, None]
        score_maxima, weighted_totals, exponent_sums = attend((score_maxima, weighted_totals, exponent_sums), scores, values_back, valid)
        moving = jnp.einsum('nhie,nhef->nhif', moving, maps_back, precision=highest)
        return (score_maxima, weighted_totals, exponent_sums, moving)
    score_maxima, weighted_totals, exponent_sums, moving = lax.fori_loop(1, block_list, advance, (score_maxima, weighted_totals, exponent_sums, query_start))
    final_output = exponent_sums / weighted_totals[..., None]
    final_output = final_output.reshape(block_list, KEY_VALUE_HEADS, query_group, TOKENS_PER_PART, HEAD_WIDTH)
    final_output = jnp.transpose(final_output, (0, 3, 1, 2, 4)).reshape(SEQUENCE_TOKENS, QUERY_HEADS, HEAD_WIDTH)
    return final_output.astype(jnp.bfloat16)
```

```python
import functools

import jax
import jax.numpy as jnp
from jax import lax
from jax.experimental import pallas as pl
from jax.experimental.pallas import tpu as pltpu
from jax.sharding import PartitionSpec as P

F32 = jnp.float32
BF16 = jnp.bfloat16
VMEM_LIMIT = 60 * 1024 * 1024
LOW = -1e30


def halves(x):
    h = x.astype(BF16)
    return h, (x - h.astype(F32)).astype(BF16)


def left_cat(x):
    h, l = halves(x)
    return jnp.concatenate([h, l, h], axis=1)


def right_rows(x):
    h, l = halves(x)
    return jnp.concatenate([h, h, l], axis=0)


def right_cols(x):
    h, l = halves(x)
    return jnp.concatenate([h, h, l], axis=1)


def mm(a, b):
    return lax.dot_general(a, b, (((1,), (0,)), ((), ())), preferred_element_type=F32)


def mm_t(a, b):
    return lax.dot_general(a, b, (((1,), (1,)), ((), ())), preferred_element_type=F32)


def dot_nn(a, b):
    return mm(left_cat(a), right_rows(b))


def dot_nt(a, b):
    return mm_t(left_cat(a), right_cols(b))


def call(kernel, out_shape, args, scratch=(), scalars=None, flops=0, nbytes=0, exps=0):
    vm = pl.BlockSpec(memory_space=pltpu.VMEM)
    sm = pl.BlockSpec(memory_space=pltpu.SMEM)
    specs = [vm] * len(args)
    if scalars is not None:
        specs = [sm] + specs
        args = [scalars] + list(args)
    outs = jax.tree.map(lambda _: vm, out_shape)
    return pl.pallas_call(
        kernel,
        out_shape=out_shape,
        in_specs=specs,
        out_specs=outs,
        scratch_shapes=list(scratch),
        compiler_params=pltpu.CompilerParams(vmem_limit_bytes=VMEM_LIMIT),
        cost_estimate=pl.CostEstimate(flops=flops, bytes_accessed=nbytes, transcendentals=exps),
    )(*args)


def block_kernel(heads, length, width, scal, *refs):
    packs = refs[:heads]
    kt_ref, v_ref, m_ref, wk_ref, yz_ref = refs[heads:]
    place = scal[0]
    rows = lax.broadcasted_iota(jnp.int32, (length, length), 0)
    cols = lax.broadcasted_iota(jnp.int32, (length, length), 1)
    eye = (rows == cols).astype(F32)
    eye_w = (
        lax.broadcasted_iota(jnp.int32, (width, width), 0)
        == lax.broadcasted_iota(jnp.int32, (width, width), 1)
    ).astype(F32)
    strict = rows > cols
    units, keys, betas, lows, xs = [], [], [], [], []
    for d in range(heads):
        k = packs[d][0:length]
        w = packs[d][2 * length : 3 * length]
        b_row = packs[d][3 * length : 3 * length + 1]
        beta = 2.0 / (1.0 + jnp.exp(-b_row))
        beta = jnp.transpose(jnp.broadcast_to(beta, (length, length)))
        unit = w / jnp.sqrt(jnp.sum(w * w, -1, keepdims=True) + 1e-06)
        gram = dot_nt(unit, unit)
        low = jnp.where(strict, beta * gram, 0.0)
        units.append(unit)
        keys.append(k)
        betas.append(beta)
        lows.append(low)
        level = (rows // 2 == cols // 2) & (rows % 2 == 1) & (cols % 2 == 0)
        xs.append(eye - jnp.where(level, low, 0.0))
    size = 2
    while size < length:
        level = (
            (rows // (2 * size) == cols // (2 * size))
            & ((rows // size) % 2 == 1)
            & ((cols // size) % 2 == 0)
        )
        part = [dot_nn(jnp.where(level, lows[d], 0.0), xs[d]) for d in range(heads)]
        part = [dot_nn(xs[d], part[d]) for d in range(heads)]
        xs = [xs[d] - part[d] for d in range(heads)]
        size *= 2
    for d in range(heads):
        slot = lax.rem(place - d + heads, heads)
        unit, k, beta = units[d], keys[d], betas[d]
        kb = k.astype(BF16)
        uh, ul = halves(unit)
        cross = mm_t(jnp.concatenate([uh, ul], axis=1), jnp.concatenate([kb, kb], axis=1))
        cross = jnp.where(strict, cross, 0.0)
        yz = dot_nn(xs[d], jnp.concatenate([beta[:, :width] * unit, beta * cross], axis=1))
        y, z = yz[:, :width], yz[:, width:]
        m_ref[slot] = eye_w - dot_nn(jnp.transpose(unit), y)
        kt_ref[slot] = k - dot_nn(jnp.transpose(z), unit)
        v_ref[slot] = packs[d][length : 2 * length]
        wk_ref[slot] = jnp.concatenate(
            [
                jnp.concatenate([uh, ul], axis=1),
                jnp.concatenate([kb, jnp.zeros_like(kb)], axis=1),
            ],
            axis=0,
        )
        yz_ref[slot] = right_rows(yz)


def section_kernel(heads, ring, width, scal, *refs):
    kts, vs, ms = refs[:ring], refs[ring : 2 * ring], refs[2 * ring : 3 * ring]
    kcat_ref, mcat_ref, vb_ref, kend_ref, vsec_ref, s_ref = refs[3 * ring : 3 * ring + 6]
    kt_s, m_s = refs[3 * ring + 6 :]
    low = scal[1]
    for r in range(ring):
        lane = lax.rem(low - r + ring, ring)
        for t in range(heads):
            b = t * ring + lane
            kt_s[b] = kts[r][t]
            vb_ref[b] = vs[r][t].astype(BF16)
            vsec_ref[b] = vs[r][t]
            kcat_ref[b] = right_cols(kts[r][t])
            mcat_ref[b] = right_rows(ms[r][t])
    eye = (
        lax.broadcasted_iota(jnp.int32, (width, width), 0)
        == lax.broadcasted_iota(jnp.int32, (width, width), 1)
    ).astype(F32)

    last = heads * ring - 1
    m_s[last] = eye

    def step(i, c):
        b = last - i
        m_s[b - 1] = mm(left_cat(m_s[b]), mcat_ref[b])
        return c

    lax.fori_loop(0, last, step, 0)
    s_ref[...] = mm(left_cat(m_s[0]), mcat_ref[0])

    def turn(b, c):
        kend_ref[b] = dot_nt(kt_s[b], m_s[b])
        return c

    lax.fori_loop(0, heads * ring, turn, 0)


def near_kernel(heads, ring, length, width, scal, *refs):
    qs = refs[:heads]
    wk_ref, yz_ref, kcat_ref, mcat_ref, vb_ref = refs[heads : heads + 5]
    qcat_ref, ml_ref, acc_ref = refs[heads + 5 : heads + 8]
    q_s, m_s, l_s = refs[heads + 8 :]
    place, low = scal[0], scal[1]
    rows = qs[0].shape[0]
    scale = width ** (-0.5)
    for d in range(heads):
        q_s[lax.rem(place - d + heads, heads)] = qs[d][...]
    token = lax.rem(lax.broadcasted_iota(jnp.int32, (rows, length), 0), length)
    causal = token >= lax.broadcasted_iota(jnp.int32, (rows, length), 1)

    def own(t, b):
        qf = q_s[t]
        q = qf.astype(BF16)
        both = mm_t(jnp.concatenate([q, q], axis=1), wk_ref[t])
        qw = jnp.where(causal, both[:, :length], 0.0)
        u = mm(left_cat(qw), yz_ref[t])
        q_s[t] = (qf - u[:, :width]) * scale
        s = jnp.where(causal, (both[:, length:] - u[:, width:]) * scale, LOW)
        top = jnp.max(s, -1, keepdims=True)
        p = jnp.where(causal, jnp.exp(s - top), 0.0)
        m_s[t] = top
        l_s[t] = jnp.sum(p, -1, keepdims=True)
        acc_ref[t] = mm(p.astype(BF16), vb_ref[b])

    def earlier(t, b):
        qc = left_cat(q_s[t])
        s = mm_t(qc, kcat_ref[b])
        old = m_s[t]
        top = jnp.maximum(old, jnp.max(s, -1, keepdims=True))
        p = jnp.exp(s - top)
        f = jnp.exp(old - top)
        m_s[t] = top
        l_s[t] = l_s[t] * f + jnp.sum(p, -1, keepdims=True)
        acc_ref[t] = acc_ref[t] * f + mm(p.astype(BF16), vb_ref[b])
        q_s[t] = mm(qc, mcat_ref[b])

    def step(i, carry):
        b = heads * ring - 1 - i
        t_b = b // ring
        lane = b - t_b * ring
        first = jnp.where(low > lane, t_b, t_b + 1)

        def body(t, c):
            earlier(t, b)
            return c

        lax.fori_loop(first, heads, body, 0)

        @pl.when(lane == low)
        def _():
            own(t_b, b)

        return carry

    lax.fori_loop(0, heads * ring, step, 0)

    def finish(t, c):
        qcat_ref[t] = left_cat(q_s[t])
        lane_id = lax.broadcasted_iota(jnp.int32, (rows, 128), 1)
        ml_ref[t] = jnp.where(lane_id < 64, m_s[t], l_s[t])
        return c

    lax.fori_loop(0, heads, finish, 0)


def move_kernel(k_ref, s_ref, out_ref):
    cat = right_cols(s_ref[...])

    def step(b, c):
        out_ref[b] = mm_t(left_cat(k_ref[b]), cat)
        return c

    lax.fori_loop(0, k_ref.shape[0], step, 0)


def far_kernel(step, last, tile, scal, q_ref, ml_ref, acc_ref, k_ref, v_ref, *refs):
    if last:
        out_ref, kc, vc = refs
    else:
        ml_out, acc_out, kc, vc = refs
    blocks, length, width = k_ref.shape
    rows = q_ref.shape[1]
    live = scal[2] >= step

    @pl.when(live)
    def _():
        def prep(b, c):
            at = pl.ds(pl.multiple_of(b * length, length), length)
            kc[at] = right_cols(k_ref[b])
            vc[at] = v_ref[b].astype(BF16)
            return c

        lax.fori_loop(0, blocks, prep, 0)

    per = rows // tile

    def body(i, c):
        t = i // per
        at = pl.ds(pl.multiple_of((i - t * per) * tile, tile), tile)
        ml = ml_ref[t, at]
        old, tot = ml[:, 0:1], ml[:, 64:65]
        acc = acc_ref[t, at]

        def store(m, l, a):
            if last:
                out_ref[t, at] = a / l
            else:
                lane_id = lax.broadcasted_iota(jnp.int32, (tile, 128), 1)
                ml_out[t, at] = jnp.where(lane_id < 64, m, l)
                acc_out[t, at] = a

        @pl.when(live)
        def _():
            s = mm_t(q_ref[t, at], kc[...])
            top = jnp.maximum(old, jnp.max(s, -1, keepdims=True))
            p = jnp.exp(s - top)
            f = jnp.exp(old - top)
            store(
                top,
                tot * f + jnp.sum(p, -1, keepdims=True),
                acc * f + mm(p.astype(BF16), vc[...]),
            )

        @pl.when(jnp.logical_not(live))
        def _():
            store(old, tot, acc)

        return c

    lax.fori_loop(0, q_ref.shape[0] * per, body, 0)


def join_kernel(heads, scal, *refs):
    out_ref = refs[heads]
    for d in range(heads):
        out_ref[lax.rem(scal[0] - d + heads, heads)] = refs[d][...].astype(BF16)


def body(query, key, value, raw_directions, beta_raw_logits):
    length, q_count, width = query.shape
    heads = key.shape[1]
    group = q_count // heads
    key_count, sec_count = lax.axis_size("key"), lax.axis_size("sec")
    ring = key_count // heads
    key_index, sec_index = lax.axis_index("key"), lax.axis_index("sec")
    place, low = key_index // ring, key_index % ring
    scal = jnp.stack([place, low, sec_index]).astype(jnp.int32)
    blocks = heads * ring
    rows = group * length

    def around(d):
        return [(k, ((k // ring + d) % heads) * ring + k % ring) for k in range(key_count)]

    def across(d):
        return [(k, (k // ring) * ring + (k % ring + d) % ring) for k in range(key_count)]

    def spread(x):
        own = [
            lax.dynamic_index_in_dim(x, lax.rem(place + d, heads), 0, keepdims=False)
            for d in range(heads)
        ]
        return [own[0]] + [lax.ppermute(own[d], "key", around(d)) for d in range(1, heads)]

    def by_head(x):
        return jnp.transpose(x.astype(F32), (1, 0, 2))

    sds = jax.ShapeDtypeStruct
    lines = jnp.transpose(beta_raw_logits, (1, 0))[:, None, :]
    lines = jnp.pad(lines, ((0, 0), (0, 7), (0, 0)))
    pack = jnp.concatenate([by_head(key), by_head(value), by_head(raw_directions), lines], axis=1)
    packs = spread(pack)
    q_heads = by_head(query).reshape(heads, rows, width)
    qs = spread(q_heads)

    cube = sds((heads, length, width), F32)
    kt, v, m, wk, yz = call(
        functools.partial(block_kernel, heads, length, width),
        (
            cube,
            cube,
            sds((heads, width, width), F32),
            sds((heads, 2 * length, 2 * width), BF16),
            sds((heads, 3 * length, width + length), BF16),
        ),
        packs,
        scalars=scal,
        flops=heads * 20 * 6 * length**3,
        nbytes=heads * 10 * length * width * 4,
    )

    def gather(x):
        return [x] + [lax.ppermute(x, "key", across(d)) for d in range(1, ring)]

    kts, vs, ms = gather(kt), gather(v), gather(m)
    full = sds((blocks, length, width), F32)
    kcat, mcat, vb, kend, vsec, smap = call(
        functools.partial(section_kernel, heads, ring, width),
        (
            sds((blocks, length, 3 * width), BF16),
            sds((blocks, 3 * width, width), BF16),
            sds((blocks, length, width), BF16),
            full,
            full,
            sds((width, width), F32),
        ),
        kts + vs + ms,
        scratch=[pltpu.VMEM((blocks, length, width), F32)] * 2,
        scalars=scal,
        flops=blocks * 12 * length**3,
        nbytes=blocks * 8 * length * width * 4,
    )
    qcat, ml, acc = call(
        functools.partial(near_kernel, heads, ring, length, width),
        (
            sds((heads, rows, 3 * width), BF16),
            sds((heads, rows, 128), F32),
            sds((heads, rows, width), F32),
        ),
        qs + [wk, yz, kcat, mcat, vb],
        scratch=[
            pltpu.VMEM((heads, rows, width), F32),
            pltpu.VMEM((heads, rows, 1), F32),
            pltpu.VMEM((heads, rows, 1), F32),
        ],
        scalars=scal,
        flops=heads * blocks // 2 * rows * width * length * 14,
        nbytes=heads * rows * width * 16,
        exps=heads * blocks // 2 * rows * length,
    )
    walk = [(s, s + 1) for s in range(sec_count - 1)]
    k_far, v_far = kend, vsec
    for step in range(1, sec_count):
        k_far = lax.ppermute(k_far, "sec", walk)
        v_far = lax.ppermute(v_far, "sec", walk)
        last = step == sec_count - 1
        outs = (sds((heads, rows, 128), F32), sds((heads, rows, width), F32))
        got = call(
            functools.partial(far_kernel, step, last, 256),
            outs[1] if last else outs,
            [qcat, ml, acc, k_far, v_far],
            scratch=[
                pltpu.VMEM((blocks * length, 3 * width), BF16),
                pltpu.VMEM((blocks * length, width), BF16),
            ],
            scalars=scal,
            flops=heads * rows * blocks * length * width * 8,
            nbytes=heads * rows * width * 16,
            exps=heads * rows * blocks * length,
        )
        if last:
            out = got
        else:
            ml, acc = got
            k_far = call(
                move_kernel,
                full,
                [k_far, smap],
                flops=blocks * 6 * length**3,
                nbytes=blocks * length * width * 8,
            )
    back = spread(out)
    joined = call(
        functools.partial(join_kernel, heads),
        sds((heads, rows, width), BF16),
        back,
        scalars=scal,
        nbytes=heads * rows * width * 6,
    )
    return jnp.transpose(joined.reshape(q_count, length, width), (1, 0, 2))


def solution(mesh):
    rows = P(("sec", "key"), None, None)
    return jax.shard_map(
        body,
        mesh=mesh,
        in_specs=(rows, rows, rows, rows, P(("sec", "key"), None)),
        out_specs=rows,
        check_vma=False,
    )
```

```python
import functools

import jax
import jax.numpy as jnp
from jax import lax
from jax.experimental import pallas as pl
from jax.experimental.pallas import tpu as pltpu
from jax.sharding import PartitionSpec as P


F32 = jnp.float32
BF16 = jnp.bfloat16
VMEM_LIMIT = 20 * 1024 * 1024
LOW = -1e30
LOG2_E = 1.4426950408889634


def halves(x):
    h = x.astype(BF16)
    return h, (x - h.astype(F32)).astype(BF16)


def left_cat(x):
    h, l = halves(x)
    return jnp.concatenate([h, l, h], axis=1)


def right_rows(x):
    h, l = halves(x)
    return jnp.concatenate([h, h, l], axis=0)


def mm(a, b):
    return lax.dot_general(a, b, (((1,), (0,)), ((), ())), preferred_element_type=F32)


def dot_nn(a, b):
    return mm(left_cat(a), right_rows(b))


def call(kernel, out_shape, args, scratch=(), scalars=None, flops=0, nbytes=0, exps=0):
    vm = pl.BlockSpec(memory_space=pltpu.VMEM)
    sm = pl.BlockSpec(memory_space=pltpu.SMEM)
    specs = [vm] * len(args)
    if scalars is not None:
        specs = [sm] + specs
        args = [scalars] + list(args)
    outs = jax.tree.map(lambda _: vm, out_shape)
    return pl.pallas_call(
        kernel,
        out_shape=out_shape,
        in_specs=specs,
        out_specs=outs,
        scratch_shapes=list(scratch),
        compiler_params=pltpu.CompilerParams(vmem_limit_bytes=VMEM_LIMIT),
        cost_estimate=pl.CostEstimate(flops=flops, bytes_accessed=nbytes, transcendentals=exps),
    )(*args)


def ident(n):
    rows = lax.broadcasted_iota(jnp.int32, (n, n), 0)
    return (rows == lax.broadcasted_iota(jnp.int32, (n, n), 1)).astype(F32)


def block_kernel(heads, length, width, scal, *refs):
    packs = refs[:heads]
    km_ref, wk_ref, yz_ref = refs[heads:]
    place = scal[0]
    rows = lax.broadcasted_iota(jnp.int32, (length, length), 0)
    cols = lax.broadcasted_iota(jnp.int32, (length, length), 1)
    eye = ident(length)
    strict = rows > cols
    units, turned, betas, lows, xs = [], [], [], [], []
    for d in range(heads):
        w = packs[d][length : 2 * length]
        b_row = packs[d][2 * length : 2 * length + 1]
        beta = 2.0 / (1.0 + jnp.exp(-b_row))
        beta = jnp.transpose(jnp.broadcast_to(beta, (length, length)))
        unit = w / jnp.sqrt(jnp.sum(w * w, -1, keepdims=True) + 1e-06)
        across = jnp.transpose(unit)
        low = jnp.where(strict, beta * dot_nn(unit, across), 0.0)
        units.append(unit)
        turned.append(across)
        betas.append(beta)
        lows.append(low)
        level = (rows // 2 == cols // 2) & (rows % 2 == 1) & (cols % 2 == 0)
        xs.append(eye - jnp.where(level, low, 0.0))
    size = 2
    while size < length:
        level = (
            (rows // (2 * size) == cols // (2 * size))
            & ((rows // size) % 2 == 1)
            & ((cols // size) % 2 == 0)
        )
        part = [dot_nn(jnp.where(level, lows[d], 0.0), xs[d]) for d in range(heads)]
        part = [dot_nn(xs[d], part[d]) for d in range(heads)]
        xs = [xs[d] - part[d] for d in range(heads)]
        size *= 2
    for d in range(heads):
        slot = lax.rem(place - d + heads, heads)
        unit, beta, across = units[d], betas[d], turned[d]
        kt = jnp.transpose(packs[d][0:length])
        kb = kt.astype(BF16)
        uh, ul = halves(unit)
        cross = mm(jnp.concatenate([uh, ul], axis=1), jnp.concatenate([kb, kb], axis=0))
        cross = jnp.where(strict, cross, 0.0)
        zy = dot_nn(xs[d], jnp.concatenate([beta * cross, beta[:, :width] * unit], axis=1))
        base = jnp.concatenate([kt, ident(width)], axis=1)
        km_ref[slot] = base - dot_nn(across, zy)
        ah, al = halves(across)
        wk_ref[slot] = jnp.concatenate(
            [
                jnp.concatenate([ah, kb], axis=1),
                jnp.concatenate([al, jnp.zeros_like(kb)], axis=1),
            ],
            axis=0,
        )
        yz_ref[slot] = right_rows(zy)


def section_kernel(heads, ring, length, scal, *refs):
    kms = refs[:ring]
    kmcat_ref, pack_ref = refs[ring:]
    low = scal[1]
    width = pack_ref.shape[0]
    blocks = heads * ring
    for r in range(ring):
        lane = lax.rem(low - r + ring, ring)
        for t in range(heads):
            kmcat_ref[t * ring + lane] = right_rows(kms[r][t])
    suffix = ident(width)
    for b in range(blocks - 1, -1, -1):
        got = mm(left_cat(suffix), kmcat_ref[b])
        pack_ref[:, b * length : (b + 1) * length] = got[:, :length]
        suffix = got[:, length:]
    pack_ref[:, blocks * length :] = suffix


def value_kernel(heads, ring, length, scal, *refs):
    vs = refs[:ring]
    vb_ref, vsec_ref = refs[ring:]
    for r in range(ring):
        lane = lax.rem(scal[1] - r + ring, ring)
        for d in range(heads):
            b = lax.rem(scal[0] - d + heads, heads) * ring + lane
            at = pl.ds(pl.multiple_of(b * length, length), length)
            vb_ref[at] = vs[r][d].astype(BF16)
            vsec_ref[at] = vs[r][d]


def near_kernel(heads, ring, length, width, scal, *refs):
    qs = refs[:heads]
    wk_ref, yz_ref, kmcat_ref, vb_ref = refs[heads : heads + 4]
    qcat_ref, ml_ref, acc_ref = refs[heads + 4 : heads + 7]
    q_s, s_s = refs[heads + 7 :]
    place, low = scal[0], scal[1]
    rows = qs[0].shape[0]
    scale = width ** (-0.5) * LOG2_E
    blocks = heads * ring
    keys = blocks * length
    token = lax.rem(lax.broadcasted_iota(jnp.int32, (rows, length), 0), length)
    causal = token >= lax.broadcasted_iota(jnp.int32, (rows, length), 1)
    lane_id = lax.broadcasted_iota(jnp.int32, (rows // 2, 128), 1)
    for d in range(heads):
        q_s[d] = qs[d][...]

    def at(b):
        return pl.ds(pl.multiple_of(b * length, length), length)

    def piece(d, carry):
        t = lax.rem(place - d + heads, heads)
        b_own = t * ring + low
        qf = q_s[d]
        q = qf.astype(BF16)
        both = mm(jnp.concatenate([q, q], axis=1), wk_ref[t])
        qw = jnp.where(causal, both[:, :length], 0.0)
        u = mm(left_cat(qw), yz_ref[t])
        q_s[d] = (qf - u[:, length:]) * scale
        s_s[:, at(b_own)] = jnp.where(causal, (both[:, length:] - u[:, :length]) * scale, LOW)

        def clear(b, c):
            s_s[:, at(b)] = jnp.full((rows, length), LOW, F32)
            return c

        lax.fori_loop(b_own + 1, blocks, clear, 0)

        def step(i, c):
            b = b_own - 1 - i
            both = mm(left_cat(q_s[d]), kmcat_ref[b])
            s_s[:, at(b)] = both[:, :length]
            q_s[d] = both[:, length:]
            return c

        lax.fori_loop(0, b_own, step, 0)
        qcat_ref[d] = left_cat(q_s[d])

        def finish(n):
            for half in range(2):
                part = slice(half * rows // 2, (half + 1) * rows // 2)
                s = s_s[part, :n]
                top = jnp.max(s, -1, keepdims=True)
                p = jnp.exp2(s - top)
                ml_ref[d, part] = jnp.where(lane_id < 64, top, jnp.sum(p, -1, keepdims=True))
                acc_ref[d, part] = mm(p.astype(BF16), vb_ref[:n])

        small = b_own < blocks // 2

        @pl.when(small)
        def _():
            finish(keys // 2)

        @pl.when(jnp.logical_not(small))
        def _():
            finish(keys)

        return carry

    lax.fori_loop(0, heads, piece, 0)


def prep_kernel(hops, scal, *refs):
    n = 2 * hops + 1
    packs, values = refs[:n], refs[n : 2 * n]
    kc_ref, vc_ref, got = refs[2 * n :]
    sec = scal[2]
    core = lax.rem(sec, 2)
    width = got.shape[0]
    keys = got.shape[1] - width
    got_map = ident(width)

    def take(dst, i):
        dst[...] = packs[i][...]

    def take_v(dist, i):
        vc_ref[dist - 1] = values[i][...].astype(BF16)

    for dist in range(1, n + 1):
        p = dist // 2
        if dist % 2 == 0:
            take(got, 2 * p - 1)
            take_v(dist, 2 * p - 1)
        else:

            @pl.when(core == 1)
            def _():
                take(got, 2 * p)
                take_v(dist, 2 * p)

            if p + 1 <= hops:

                @pl.when(core == 0)
                def _():
                    take(got, 2 * p + 2)
                    take_v(dist, 2 * p + 2)

        moved = mm(left_cat(got_map), right_rows(got[...])) if dist > 1 else got[...]
        kc_ref[dist - 1] = right_rows(moved[:, :keys])
        got_map = moved[:, keys:]


def far_kernel(first, parts, scal, q_ref, ml_ref, acc_ref, k_ref, v_ref, *refs):
    count = len(refs) - 3
    outs = refs[:count]
    m_s, l_s, a_s = refs[count:]
    rows = q_ref.shape[1]
    size = rows // parts
    spots = [(d, p) for d in range(count) for p in range(parts)]
    for i, (d, p) in enumerate(spots):
        part = slice(p * size, (p + 1) * size)
        m_s[i] = ml_ref[first + d, part, 0:1]
        l_s[i] = ml_ref[first + d, part, 64:65]
        a_s[i] = acc_ref[first + d, part]

    def scores(i, sec):
        d, p = spots[i]
        return mm(q_ref[first + d, p * size : (p + 1) * size], k_ref[sec])

    def step(sec, c):
        s = scores(0, sec)
        for i in range(len(spots)):
            coming = scores(i + 1, sec) if i + 1 < len(spots) else None
            old = m_s[i]
            top = jnp.maximum(old, jnp.max(s, -1, keepdims=True))
            p = jnp.exp2(s - top)
            f = jnp.exp2(old - top)
            m_s[i] = top
            l_s[i] = l_s[i] * f + jnp.sum(p, -1, keepdims=True)
            a_s[i] = a_s[i] * f + mm(p.astype(BF16), v_ref[sec])
            s = coming
        return c

    lax.fori_loop(0, jnp.minimum(scal[2], k_ref.shape[0]), step, 0)
    for i, (d, p) in enumerate(spots):
        outs[d][p * size : (p + 1) * size] = a_s[i] / l_s[i]


def join_kernel(heads, scal, *refs):
    out_ref = refs[heads]
    for d in range(heads):
        out_ref[lax.rem(scal[0] + d, heads)] = refs[d][...].astype(BF16)


def steps(query, key, value, raw_directions, beta_raw_logits):
    length, q_count, width = query.shape
    heads = key.shape[1]
    group = q_count // heads
    key_count, sec_count = lax.axis_size("key"), lax.axis_size("sec")
    ring = key_count // heads
    hops = sec_count // 2 - 1
    key_index, sec_index = lax.axis_index("key"), lax.axis_index("sec")
    place, low = key_index // ring, key_index % ring
    scal = jnp.stack([place, low, sec_index]).astype(jnp.int32)
    blocks = heads * ring
    rows = group * length
    keys = blocks * length

    def around(d):
        return [(k, ((k // ring + d) % heads) * ring + k % ring) for k in range(key_count)]

    def across(d):
        return [(k, (k // ring) * ring + (k % ring + d) % ring) for k in range(key_count)]

    def send(x, axis, pairs):
        return lax.ppermute(x, axis, pairs)

    def chunks(x):
        return [
            lax.dynamic_index_in_dim(x, lax.rem(place + d, heads), 0, keepdims=False)
            for d in range(heads)
        ]

    def deal(own):
        return [own[0]] + [send(own[d], "key", around(d)) for d in range(1, heads)]

    def gather(x):
        return [x] + [send(x, "key", across(d)) for d in range(1, ring)]

    def by_head(x):
        return jnp.transpose(x.astype(F32), (1, 0, 2))

    sds = jax.ShapeDtypeStruct
    lines = jnp.transpose(beta_raw_logits, (1, 0))[:, None, :]
    lines = jnp.pad(lines, ((0, 0), (0, 7), (0, 0)))
    pack = jnp.concatenate([by_head(key), by_head(raw_directions), lines], axis=1)
    packs = deal(chunks(pack))
    values = deal(chunks(by_head(value)))
    qs = deal(chunks(by_head(query).reshape(heads, rows, width)))

    km, wk, yz = call(
        functools.partial(block_kernel, heads, length, width),
        (
            sds((heads, width, length + width), F32),
            sds((heads, 2 * width, 2 * length), BF16),
            sds((heads, 3 * length, length + width), BF16),
        ),
        packs,
        scalars=scal,
        flops=heads * 20 * 6 * length**3,
        nbytes=heads * 10 * length * width * 4,
    )

    v_own = jnp.stack(values)

    def arrange(parts):
        return call(
            functools.partial(value_kernel, heads, ring, length),
            (sds((keys, width), BF16), sds((keys, width), F32)),
            parts,
            scalars=scal,
            nbytes=blocks * length * width * 10,
        )

    v_parts = gather(v_own)
    km_parts = gather(km)
    vb, vsec = arrange(v_parts)
    kmcat, packet = call(
        functools.partial(section_kernel, heads, ring, length),
        (
            sds((blocks, 3 * width, length + width), BF16),
            sds((width, blocks * length + width), F32),
        ),
        km_parts,
        scalars=scal,
        flops=blocks * 12 * length**3,
        nbytes=blocks * 8 * length * width * 4,
    )

    pair = [(s, s ^ 1) for s in range(sec_count)]
    rise = [(s, s + 1) for s in range(0, sec_count, 2)]
    v_far = [send(vsec, "sec", rise)]
    k_far = [send(packet, "sec", rise)]
    for p in range(1, hops + 1):
        line = [(s, s + 2 * p) for s in range(sec_count - 2 * p)]
        v_got = arrange(gather(send(v_own, "sec", line)))[1]
        k_got = send(packet, "sec", line)
        v_far += [v_got, send(v_got, "sec", pair)]
        k_far += [k_got, send(k_got, "sec", pair)]
    qcat, ml, acc = call(
        functools.partial(near_kernel, heads, ring, length, width),
        (
            sds((heads, rows, 3 * width), BF16),
            sds((heads, rows, 128), F32),
            sds((heads, rows, width), F32),
        ),
        qs + [wk, yz, kmcat, vb],
        scratch=[pltpu.VMEM((heads, rows, width), F32), pltpu.VMEM((rows, keys), F32)],
        scalars=scal,
        flops=heads * blocks // 2 * rows * width * length * 14,
        nbytes=heads * rows * width * 16,
        exps=heads * blocks // 2 * rows * length,
    )
    far_count = 2 * hops + 1
    kc, vc = call(
        functools.partial(prep_kernel, hops),
        (sds((far_count, 3 * width, keys), BF16), sds((far_count, keys, width), BF16)),
        k_far + v_far,
        scratch=[pltpu.VMEM((width, keys + width), F32)],
        scalars=scal,
        flops=far_count * width * width * keys * 6,
        nbytes=far_count * keys * width * 16,
    )
    parts = 2

    def far(first, count):
        got = call(
            functools.partial(far_kernel, first, parts),
            (sds((rows, width), F32),) * count,
            [qcat, ml, acc, kc, vc],
            scratch=[
                pltpu.VMEM((count * parts, rows // parts, 1), F32),
                pltpu.VMEM((count * parts, rows // parts, 1), F32),
                pltpu.VMEM((count * parts, rows // parts, width), F32),
            ],
            scalars=scal,
            flops=count * rows * far_count * keys * width * 8,
            nbytes=count * rows * width * 20 + far_count * keys * width * 8,
            exps=count * rows * far_count * keys,
        )
        return list(got)

    back = [None] * heads
    for d in [heads // 2] + [d for d in range(1, heads) if d != heads // 2] + [0]:
        (piece,) = far(d, 1)
        back[d] = send(piece, "key", around(-d)) if d else piece
    joined = call(
        functools.partial(join_kernel, heads),
        sds((heads, rows, width), BF16),
        back,
        scalars=scal,
        nbytes=heads * rows * width * 6,
    )
    return jnp.transpose(joined.reshape(q_count, length, width), (1, 0, 2))


def solution(mesh):
    rows = P(("sec", "key"), None, None)
    return jax.shard_map(
        steps,
        mesh=mesh,
        in_specs=(rows, rows, rows, rows, P(("sec", "key"), None)),
        out_specs=rows,
        check_vma=False,
    )
```

```python
import functools

import jax
import jax.numpy as jnp
from jax import lax
from jax.experimental import pallas as pl
from jax.experimental.pallas import tpu as pltpu
from jax.sharding import PartitionSpec as P


F32 = jnp.float32
BF16 = jnp.bfloat16
VMEM_LIMIT = 20 * 1024 * 1024
LOW = -1e30
LOG2_E = 1.4426950408889634


def halves(x):
    h = x.astype(BF16)
    return h, (x - h.astype(F32)).astype(BF16)


def left_cat(x):
    h, l = halves(x)
    return jnp.concatenate([h, l, h], axis=1)


def right_rows(x):
    h, l = halves(x)
    return jnp.concatenate([h, h, l], axis=0)


def mm(a, b):
    return lax.dot_general(a, b, (((1,), (0,)), ((), ())), preferred_element_type=F32)


def dot_nn(a, b):
    return mm(left_cat(a), right_rows(b))


def call(kernel, out_shape, args, scratch=(), scalars=None, flops=0, nbytes=0, exps=0):
    vm = pl.BlockSpec(memory_space=pltpu.VMEM)
    sm = pl.BlockSpec(memory_space=pltpu.SMEM)
    specs = [vm] * len(args)
    if scalars is not None:
        specs = [sm] + specs
        args = [scalars] + list(args)
    outs = jax.tree.map(lambda _: vm, out_shape)
    return pl.pallas_call(
        kernel,
        out_shape=out_shape,
        in_specs=specs,
        out_specs=outs,
        scratch_shapes=list(scratch),
        compiler_params=pltpu.CompilerParams(vmem_limit_bytes=VMEM_LIMIT),
        cost_estimate=pl.CostEstimate(flops=flops, bytes_accessed=nbytes, transcendentals=exps),
    )(*args)


def ident(n):
    rows = lax.broadcasted_iota(jnp.int32, (n, n), 0)
    return (rows == lax.broadcasted_iota(jnp.int32, (n, n), 1)).astype(F32)


def block_kernel(heads, length, width, scal, *refs):
    packs = refs[:heads]
    km_ref, wk_ref, yz_ref = refs[heads:]
    place = scal[0]
    rows = lax.broadcasted_iota(jnp.int32, (length, length), 0)
    cols = lax.broadcasted_iota(jnp.int32, (length, length), 1)
    eye = ident(length)
    strict = rows > cols
    units, turned, betas, lows, xs = [], [], [], [], []
    for d in range(heads):
        w = packs[d][length : 2 * length]
        b_row = packs[d][2 * length : 2 * length + 1]
        beta = 2.0 / (1.0 + jnp.exp(-b_row))
        beta = jnp.transpose(jnp.broadcast_to(beta, (length, length)))
        unit = w / jnp.sqrt(jnp.sum(w * w, -1, keepdims=True) + 1e-06)
        across = jnp.transpose(unit)
        low = jnp.where(strict, beta * dot_nn(unit, across), 0.0)
        units.append(unit)
        turned.append(across)
        betas.append(beta)
        lows.append(low)
        level = (rows // 2 == cols // 2) & (rows % 2 == 1) & (cols % 2 == 0)
        xs.append(eye - jnp.where(level, low, 0.0))
    size = 2
    while size < length:
        level = (
            (rows // (2 * size) == cols // (2 * size))
            & ((rows // size) % 2 == 1)
            & ((cols // size) % 2 == 0)
        )
        part = [dot_nn(jnp.where(level, lows[d], 0.0), xs[d]) for d in range(heads)]
        part = [dot_nn(xs[d], part[d]) for d in range(heads)]
        xs = [xs[d] - part[d] for d in range(heads)]
        size *= 2
    for d in range(heads):
        slot = lax.rem(place - d + heads, heads)
        unit, beta, across = units[d], betas[d], turned[d]
        kt = jnp.transpose(packs[d][0:length])
        kb = kt.astype(BF16)
        uh, ul = halves(unit)
        cross = mm(jnp.concatenate([uh, ul], axis=1), jnp.concatenate([kb, kb], axis=0))
        cross = jnp.where(strict, cross, 0.0)
        zy = dot_nn(xs[d], jnp.concatenate([beta * cross, beta[:, :width] * unit], axis=1))
        base = jnp.concatenate([kt, ident(width)], axis=1)
        km_ref[slot] = base - dot_nn(across, zy)
        ah, al = halves(across)
        wk_ref[slot] = jnp.concatenate(
            [
                jnp.concatenate([ah, kb], axis=1),
                jnp.concatenate([al, jnp.zeros_like(kb)], axis=1),
            ],
            axis=0,
        )
        yz_ref[slot] = right_rows(zy)


def section_kernel(heads, ring, length, scal, *refs):
    kms = refs[:ring]
    kmcat_ref, pack_ref = refs[ring:]
    low = scal[1]
    width = pack_ref.shape[0]
    blocks = heads * ring
    for r in range(ring):
        lane = lax.rem(low - r + ring, ring)
        for t in range(heads):
            kmcat_ref[t * ring + lane] = right_rows(kms[r][t])
    suffix = ident(width)
    for b in range(blocks - 1, -1, -1):
        got = mm(left_cat(suffix), kmcat_ref[b])
        pack_ref[:, b * length : (b + 1) * length] = got[:, :length]
        suffix = got[:, length:]
    pack_ref[:, blocks * length :] = suffix


def value_kernel(heads, ring, length, scal, *refs):
    vs = refs[:ring]
    vb_ref, vsec_ref = refs[ring:]
    for r in range(ring):
        lane = lax.rem(scal[1] - r + ring, ring)
        for d in range(heads):
            b = lax.rem(scal[0] - d + heads, heads) * ring + lane
            at = pl.ds(pl.multiple_of(b * length, length), length)
            vb_ref[at] = vs[r][d].astype(BF16)
            vsec_ref[at] = vs[r][d]


def near_kernel(d, heads, ring, length, width, scal, q_ref, *refs):
    wk_ref, yz_ref, kmcat_ref, vb_ref, qcat_ref, ml_ref, acc_ref, q_s, s_s = refs
    place, low = scal[0], scal[1]
    rows = q_ref.shape[0]
    scale = width ** (-0.5) * LOG2_E
    blocks = heads * ring
    keys = blocks * length
    token = lax.rem(lax.broadcasted_iota(jnp.int32, (rows, length), 0), length)
    causal = token >= lax.broadcasted_iota(jnp.int32, (rows, length), 1)
    lane_id = lax.broadcasted_iota(jnp.int32, (rows // 2, 128), 1)

    def at(b):
        return pl.ds(pl.multiple_of(b * length, length), length)

    t = lax.rem(place - d + heads, heads)
    b_own = t * ring + low
    qf = q_ref[...]
    q = qf.astype(BF16)
    both = mm(jnp.concatenate([q, q], axis=1), wk_ref[t])
    qw = jnp.where(causal, both[:, :length], 0.0)
    u = mm(left_cat(qw), yz_ref[t])
    q_s[...] = (qf - u[:, length:]) * scale
    s_s[:, at(b_own)] = jnp.where(causal, (both[:, length:] - u[:, :length]) * scale, LOW)

    def clear(b, c):
        s_s[:, at(b)] = jnp.full((rows, length), LOW, F32)
        return c

    lax.fori_loop(b_own + 1, blocks, clear, 0)

    def step(i, c):
        b = b_own - 1 - i
        both = mm(left_cat(q_s[...]), kmcat_ref[b])
        s_s[:, at(b)] = both[:, :length]
        q_s[...] = both[:, length:]
        return c

    lax.fori_loop(0, b_own, step, 0)
    qcat_ref[...] = left_cat(q_s[...])

    def finish(n):
        for half in range(2):
            part = slice(half * rows // 2, (half + 1) * rows // 2)
            s = s_s[part, :n]
            top = jnp.max(s, -1, keepdims=True)
            p = jnp.exp2(s - top)
            ml_ref[part] = jnp.where(lane_id < 64, top, jnp.sum(p, -1, keepdims=True))
            acc_ref[part] = mm(p.astype(BF16), vb_ref[:n])

    small = b_own < blocks // 2

    @pl.when(small)
    def _():
        finish(keys // 2)

    @pl.when(jnp.logical_not(small))
    def _():
        finish(keys)


def prep_kernel(hops, scal, *refs):
    n = 2 * hops + 1
    packs, values = refs[:n], refs[n : 2 * n]
    kc_ref, vc_ref, got = refs[2 * n :]
    sec = scal[2]
    core = lax.rem(sec, 2)
    width = got.shape[0]
    keys = got.shape[1] - width
    got_map = ident(width)

    def take(dst, i):
        dst[...] = packs[i][...]

    def take_v(dist, i):
        vc_ref[dist - 1] = values[i][...].astype(BF16)

    for dist in range(1, n + 1):
        p = dist // 2
        if dist % 2 == 0:
            take(got, 2 * p - 1)
            take_v(dist, 2 * p - 1)
        else:

            @pl.when(core == 1)
            def _():
                take(got, 2 * p)
                take_v(dist, 2 * p)

            if p + 1 <= hops:

                @pl.when(core == 0)
                def _():
                    take(got, 2 * p + 2)
                    take_v(dist, 2 * p + 2)

        moved = mm(left_cat(got_map), right_rows(got[...])) if dist > 1 else got[...]
        kc_ref[dist - 1] = right_rows(moved[:, :keys])
        got_map = moved[:, keys:]


def far_kernel(parts, scal, q_ref, ml_ref, acc_ref, k_ref, v_ref, out_ref, m_s, l_s, a_s):
    size = q_ref.shape[0] // parts
    spots = [slice(p * size, (p + 1) * size) for p in range(parts)]
    for i, part in enumerate(spots):
        m_s[i] = ml_ref[part, 0:1]
        l_s[i] = ml_ref[part, 64:65]
        a_s[i] = acc_ref[part]

    def step(sec, c):
        s = mm(q_ref[spots[0]], k_ref[sec])
        for i in range(parts):
            coming = mm(q_ref[spots[i + 1]], k_ref[sec]) if i + 1 < parts else None
            old = m_s[i]
            top = jnp.maximum(old, jnp.max(s, -1, keepdims=True))
            p = jnp.exp2(s - top)
            f = jnp.exp2(old - top)
            m_s[i] = top
            l_s[i] = l_s[i] * f + jnp.sum(p, -1, keepdims=True)
            a_s[i] = a_s[i] * f + mm(p.astype(BF16), v_ref[sec])
            s = coming
        return c

    lax.fori_loop(0, jnp.minimum(scal[2], k_ref.shape[0]), step, 0)
    for i, part in enumerate(spots):
        out_ref[part] = a_s[i] / l_s[i]


def join_kernel(heads, scal, *refs):
    out_ref = refs[heads]
    for d in range(heads):
        out_ref[lax.rem(scal[0] + d, heads)] = refs[d][...].astype(BF16)


def steps(query, key, value, raw_directions, beta_raw_logits):
    length, q_count, width = query.shape
    heads = key.shape[1]
    group = q_count // heads
    key_count, sec_count = lax.axis_size("key"), lax.axis_size("sec")
    ring = key_count // heads
    hops = sec_count // 2 - 1
    key_index, sec_index = lax.axis_index("key"), lax.axis_index("sec")
    place, low = key_index // ring, key_index % ring
    scal = jnp.stack([place, low, sec_index]).astype(jnp.int32)
    blocks = heads * ring
    rows = group * length
    keys = blocks * length

    def around(d):
        return [(k, ((k // ring + d) % heads) * ring + k % ring) for k in range(key_count)]

    def across(d):
        return [(k, (k // ring) * ring + (k % ring + d) % ring) for k in range(key_count)]

    def chunks(x):
        return [
            lax.dynamic_index_in_dim(x, lax.rem(place + d, heads), 0, keepdims=False)
            for d in range(heads)
        ]

    def deal(own):
        return [own[0]] + [
            lax.ppermute(own[d], "key", around(d)) for d in range(1, heads)
        ]

    def gather(x):
        return [x] + [lax.ppermute(x, "key", across(d)) for d in range(1, ring)]

    def by_head(x):
        return jnp.transpose(x.astype(F32), (1, 0, 2))

    sds = jax.ShapeDtypeStruct
    lines = jnp.transpose(beta_raw_logits, (1, 0))[:, None, :]
    lines = jnp.pad(lines, ((0, 0), (0, 7), (0, 0)))
    pack = jnp.concatenate([by_head(key), by_head(raw_directions), lines], axis=1)
    packs = deal(chunks(pack))
    values = deal(chunks(by_head(value)))
    qs = deal(chunks(by_head(query).reshape(heads, rows, width)))

    km, wk, yz = call(
        functools.partial(block_kernel, heads, length, width),
        (
            sds((heads, width, length + width), F32),
            sds((heads, 2 * width, 2 * length), BF16),
            sds((heads, 3 * length, length + width), BF16),
        ),
        packs,
        scalars=scal,
        flops=heads * 20 * 6 * length**3,
        nbytes=heads * 10 * length * width * 4,
    )

    v_own = jnp.stack(values)

    def arrange(parts):
        return call(
            functools.partial(value_kernel, heads, ring, length),
            (sds((keys, width), BF16), sds((keys, width), F32)),
            parts,
            scalars=scal,
            nbytes=blocks * length * width * 10,
        )

    v_parts = gather(v_own)
    km_parts = gather(km)
    vb, vsec = arrange(v_parts)
    kmcat, packet = call(
        functools.partial(section_kernel, heads, ring, length),
        (
            sds((blocks, 3 * width, length + width), BF16),
            sds((width, blocks * length + width), F32),
        ),
        km_parts,
        scalars=scal,
        flops=blocks * 12 * length**3,
        nbytes=blocks * 8 * length * width * 4,
    )

    pair = [(s, s ^ 1) for s in range(sec_count)]
    rise = [(s, s + 1) for s in range(0, sec_count, 2)]
    v_far = [lax.ppermute(vsec, "sec", rise)]
    k_far = [lax.ppermute(packet, "sec", rise)]
    for p in range(1, hops + 1):
        line = [(s, s + 2 * p) for s in range(sec_count - 2 * p)]
        v_got = arrange(gather(lax.ppermute(v_own, "sec", line)))[1]
        k_got = lax.ppermute(packet, "sec", line)
        v_far += [v_got, lax.ppermute(v_got, "sec", pair)]
        k_far += [k_got, lax.ppermute(k_got, "sec", pair)]

    def near(d):
        return call(
            functools.partial(near_kernel, d, heads, ring, length, width),
            (sds((rows, 3 * width), BF16), sds((rows, 128), F32), sds((rows, width), F32)),
            [qs[d], wk, yz, kmcat, vb],
            scratch=[pltpu.VMEM((rows, width), F32), pltpu.VMEM((rows, keys), F32)],
            scalars=scal,
            flops=blocks // 2 * rows * width * length * 14,
            nbytes=rows * width * 16,
            exps=blocks // 2 * rows * length,
        )

    order = [heads // 2] + [d for d in range(1, heads) if d != heads // 2] + [0]
    found = {d: near(d) for d in [0] + order[:-1]}
    far_count = 2 * hops + 1
    kc, vc = call(
        functools.partial(prep_kernel, hops),
        (sds((far_count, 3 * width, keys), BF16), sds((far_count, keys, width), BF16)),
        k_far + v_far,
        scratch=[pltpu.VMEM((width, keys + width), F32)],
        scalars=scal,
        flops=far_count * width * width * keys * 6,
        nbytes=far_count * keys * width * 16,
    )
    parts = 2

    def far(d):
        return call(
            functools.partial(far_kernel, parts),
            sds((rows, width), F32),
            list(found[d]) + [kc, vc],
            scratch=[
                pltpu.VMEM((parts, rows // parts, 1), F32),
                pltpu.VMEM((parts, rows // parts, 1), F32),
                pltpu.VMEM((parts, rows // parts, width), F32),
            ],
            scalars=scal,
            flops=rows * far_count * keys * width * 8,
            nbytes=rows * width * 20 + far_count * keys * width * 8,
            exps=rows * far_count * keys,
        )

    back = [None] * heads
    for d in order:
        piece = far(d)
        back[d] = lax.ppermute(piece, "key", around(-d)) if d else piece
    joined = call(
        functools.partial(join_kernel, heads),
        sds((heads, rows, width), BF16),
        back,
        scalars=scal,
        nbytes=heads * rows * width * 6,
    )
    return jnp.transpose(joined.reshape(q_count, length, width), (1, 0, 2))


def solution(mesh):
    rows = P(("sec", "key"), None, None)
    return jax.shard_map(
        steps,
        mesh=mesh,
        in_specs=(rows, rows, rows, rows, P(("sec", "key"), None)),
        out_specs=rows,
        check_vma=False,
    )
```

```python
import functools

import jax
import jax.numpy as jnp
from jax import lax
from jax.experimental import pallas as pl
from jax.experimental.pallas import tpu as pltpu
from jax.sharding import PartitionSpec as P


F32 = jnp.float32
BF16 = jnp.bfloat16
VMEM_LIMIT = 20 * 1024 * 1024
LOW = -1e30
LOG2_E = 1.4426950408889634


def halves(x):
    h = x.astype(BF16)
    return h, (x - h.astype(F32)).astype(BF16)


def left_cat(x):
    h, l = halves(x)
    return jnp.concatenate([h, l, h], axis=1)


def right_rows(x):
    h, l = halves(x)
    return jnp.concatenate([h, h, l], axis=0)


def mm(a, b):
    return lax.dot_general(a, b, (((1,), (0,)), ((), ())), preferred_element_type=F32)


def dot_nn(a, b):
    return mm(left_cat(a), right_rows(b))


def call(kernel, out_shape, args, scratch=(), scalars=None, flops=0, nbytes=0, exps=0):
    vm = pl.BlockSpec(memory_space=pltpu.VMEM)
    sm = pl.BlockSpec(memory_space=pltpu.SMEM)
    specs = [vm] * len(args)
    if scalars is not None:
        specs = [sm] + specs
        args = [scalars] + list(args)
    outs = jax.tree.map(lambda _: vm, out_shape)
    return pl.pallas_call(
        kernel,
        out_shape=out_shape,
        in_specs=specs,
        out_specs=outs,
        scratch_shapes=list(scratch),
        compiler_params=pltpu.CompilerParams(vmem_limit_bytes=VMEM_LIMIT),
        cost_estimate=pl.CostEstimate(flops=flops, bytes_accessed=nbytes, transcendentals=exps),
    )(*args)


def ident(n):
    rows = lax.broadcasted_iota(jnp.int32, (n, n), 0)
    return (rows == lax.broadcasted_iota(jnp.int32, (n, n), 1)).astype(F32)


def block_kernel(heads, length, width, scal, *refs):
    packs = refs[:heads]
    km_ref, wk_ref, yz_ref = refs[heads:]
    place = scal[0]
    rows = lax.broadcasted_iota(jnp.int32, (length, length), 0)
    cols = lax.broadcasted_iota(jnp.int32, (length, length), 1)
    eye = ident(length)
    strict = rows > cols
    units, turned, betas, lows, xs = [], [], [], [], []
    for d in range(heads):
        w = packs[d][length : 2 * length]
        b_row = packs[d][2 * length : 2 * length + 1]
        beta = 2.0 / (1.0 + jnp.exp(-b_row))
        beta = jnp.transpose(jnp.broadcast_to(beta, (length, length)))
        unit = w / jnp.sqrt(jnp.sum(w * w, -1, keepdims=True) + 1e-06)
        across = jnp.transpose(unit)
        low = jnp.where(strict, beta * dot_nn(unit, across), 0.0)
        units.append(unit)
        turned.append(across)
        betas.append(beta)
        lows.append(low)
        level = (rows // 2 == cols // 2) & (rows % 2 == 1) & (cols % 2 == 0)
        xs.append(eye - jnp.where(level, low, 0.0))
    size = 2
    while size < length:
        level = (
            (rows // (2 * size) == cols // (2 * size))
            & ((rows // size) % 2 == 1)
            & ((cols // size) % 2 == 0)
        )
        part = [dot_nn(jnp.where(level, lows[d], 0.0), xs[d]) for d in range(heads)]
        part = [dot_nn(xs[d], part[d]) for d in range(heads)]
        xs = [xs[d] - part[d] for d in range(heads)]
        size *= 2
    for d in range(heads):
        slot = lax.rem(place - d + heads, heads)
        unit, beta, across = units[d], betas[d], turned[d]
        kt = jnp.transpose(packs[d][0:length])
        kb = kt.astype(BF16)
        uh, ul = halves(unit)
        cross = mm(jnp.concatenate([uh, ul], axis=1), jnp.concatenate([kb, kb], axis=0))
        cross = jnp.where(strict, cross, 0.0)
        zy = dot_nn(xs[d], jnp.concatenate([beta * cross, beta[:, :width] * unit], axis=1))
        base = jnp.concatenate([kt, ident(width)], axis=1)
        km_ref[slot] = base - dot_nn(across, zy)
        ah, al = halves(across)
        wk_ref[slot] = jnp.concatenate(
            [
                jnp.concatenate([ah, kb], axis=1),
                jnp.concatenate([al, jnp.zeros_like(kb)], axis=1),
            ],
            axis=0,
        )
        yz_ref[slot] = right_rows(zy)


def section_kernel(heads, ring, length, scal, *refs):
    kms = refs[:ring]
    kmcat_ref, pack_ref = refs[ring:]
    low = scal[1]
    width = pack_ref.shape[0]
    blocks = heads * ring
    for r in range(ring):
        lane = lax.rem(low - r + ring, ring)
        for t in range(heads):
            kmcat_ref[t * ring + lane] = right_rows(kms[r][t])
    suffix = ident(width)
    for b in range(blocks - 1, -1, -1):
        got = mm(left_cat(suffix), kmcat_ref[b])
        pack_ref[:, b * length : (b + 1) * length] = got[:, :length]
        suffix = got[:, length:]
    pack_ref[:, blocks * length :] = suffix


def lay_values(heads, ring, length, scal, ref, store):
    for r in range(ring):
        lane = lax.rem(scal[1] - r + ring, ring)
        for d in range(heads):
            b = lax.rem(scal[0] - d + heads, heads) * ring + lane
            store(pl.ds(pl.multiple_of(b * length, length), length), ref[r, d].astype(BF16))


def value_kernel(heads, ring, length, scal, v_ref, vb_ref):
    def store(at, x):
        vb_ref[at] = x

    lay_values(heads, ring, length, scal, v_ref, store)


def near_kernel(d, heads, ring, length, width, scal, q_ref, *refs):
    wk_ref, yz_ref, kmcat_ref, vb_ref, qcat_ref, ml_ref, acc_ref, q_s, s_s = refs
    place, low = scal[0], scal[1]
    rows = q_ref.shape[0]
    scale = width ** (-0.5) * LOG2_E
    blocks = heads * ring
    keys = blocks * length
    token = lax.rem(lax.broadcasted_iota(jnp.int32, (rows, length), 0), length)
    causal = token >= lax.broadcasted_iota(jnp.int32, (rows, length), 1)
    lane_id = lax.broadcasted_iota(jnp.int32, (rows // 2, 128), 1)

    def at(b):
        return pl.ds(pl.multiple_of(b * length, length), length)

    t = lax.rem(place - d + heads, heads)
    b_own = t * ring + low
    qf = q_ref[...]
    q = qf.astype(BF16)
    both = mm(jnp.concatenate([q, q], axis=1), wk_ref[t])
    qw = jnp.where(causal, both[:, :length], 0.0)
    u = mm(left_cat(qw), yz_ref[t])
    q_s[...] = (qf - u[:, length:]) * scale
    s_s[:, at(b_own)] = jnp.where(causal, (both[:, length:] - u[:, :length]) * scale, LOW)

    def clear(b, c):
        s_s[:, at(b)] = jnp.full((rows, length), LOW, F32)
        return c

    lax.fori_loop(b_own + 1, blocks, clear, 0)

    def step(i, c):
        b = b_own - 1 - i
        both = mm(left_cat(q_s[...]), kmcat_ref[b])
        s_s[:, at(b)] = both[:, :length]
        q_s[...] = both[:, length:]
        return c

    lax.fori_loop(0, b_own, step, 0)
    qcat_ref[...] = left_cat(q_s[...])

    def finish(n):
        for half in range(2):
            part = slice(half * rows // 2, (half + 1) * rows // 2)
            s = s_s[part, :n]
            top = jnp.max(s, -1, keepdims=True)
            p = jnp.exp2(s - top)
            ml_ref[part] = jnp.where(lane_id < 64, top, jnp.sum(p, -1, keepdims=True))
            acc_ref[part] = mm(p.astype(BF16), vb_ref[:n])

    small = b_own < blocks // 2

    @pl.when(small)
    def _():
        finish(keys // 2)

    @pl.when(jnp.logical_not(small))
    def _():
        finish(keys)


def prep_kernel(hops, heads, ring, length, scal, *refs):
    n = 2 * hops + 1
    packs, values = refs[:n], refs[n : 2 * n]
    kc_ref, vc_ref, got = refs[2 * n :]
    sec = scal[2]
    core = lax.rem(sec, 2)
    width = got.shape[0]
    keys = got.shape[1] - width
    got_map = ident(width)

    def take(dst, i):
        dst[...] = packs[i][...]

    def take_v(dist, i):
        def store(at, x):
            vc_ref[dist - 1, at] = x

        lay_values(heads, ring, length, scal, values[i], store)

    for dist in range(1, n + 1):
        p = dist // 2
        if dist % 2 == 0:
            take(got, 2 * p - 1)
            take_v(dist, 2 * p - 1)
        else:

            @pl.when(core == 1)
            def _():
                take(got, 2 * p)
                take_v(dist, 2 * p)

            if p + 1 <= hops:

                @pl.when(core == 0)
                def _():
                    take(got, 2 * p + 2)
                    take_v(dist, 2 * p + 2)

        moved = mm(left_cat(got_map), right_rows(got[...])) if dist > 1 else got[...]
        kc_ref[dist - 1] = right_rows(moved[:, :keys])
        got_map = moved[:, keys:]


def far_kernel(parts, scal, q_ref, ml_ref, acc_ref, k_ref, v_ref, out_ref, m_s, l_s, a_s):
    size = q_ref.shape[0] // parts
    spots = [slice(p * size, (p + 1) * size) for p in range(parts)]
    for i, part in enumerate(spots):
        m_s[i] = ml_ref[part, 0:1]
        l_s[i] = ml_ref[part, 64:65]
        a_s[i] = acc_ref[part]

    def step(sec, c):
        s = mm(q_ref[spots[0]], k_ref[sec])
        for i in range(parts):
            coming = mm(q_ref[spots[i + 1]], k_ref[sec]) if i + 1 < parts else None
            old = m_s[i]
            top = jnp.maximum(old, jnp.max(s, -1, keepdims=True))
            p = jnp.exp2(s - top)
            f = jnp.exp2(old - top)
            m_s[i] = top
            l_s[i] = l_s[i] * f + jnp.sum(p, -1, keepdims=True)
            a_s[i] = a_s[i] * f + mm(p.astype(BF16), v_ref[sec])
            s = coming
        return c

    lax.fori_loop(0, jnp.minimum(scal[2], k_ref.shape[0]), step, 0)
    for i, part in enumerate(spots):
        out_ref[part] = a_s[i] / l_s[i]


def join_kernel(heads, group, scal, *refs):
    out_ref, held = refs[heads:]
    length = out_ref.shape[0]
    for d in range(heads):
        at = lax.rem(scal[0] + d, heads)
        for g in range(group):
            held[at * group + g] = refs[d][g * length : (g + 1) * length]
    out_ref[...] = jnp.swapaxes(held[...], 0, 1).astype(BF16)


def steps(query, key, value, raw_directions, beta_raw_logits):
    length, q_count, width = query.shape
    heads = key.shape[1]
    group = q_count // heads
    key_count, sec_count = lax.axis_size("key"), lax.axis_size("sec")
    ring = key_count // heads
    hops = sec_count // 2 - 1
    key_index, sec_index = lax.axis_index("key"), lax.axis_index("sec")
    place, low = key_index // ring, key_index % ring
    scal = jnp.stack([place, low, sec_index]).astype(jnp.int32)
    blocks = heads * ring
    rows = group * length
    keys = blocks * length

    def around(d):
        return [(k, ((k // ring + d) % heads) * ring + k % ring) for k in range(key_count)]

    def across(d):
        return [(k, (k // ring) * ring + (k % ring + d) % ring) for k in range(key_count)]

    def chunks(x):
        return [
            lax.dynamic_index_in_dim(x, lax.rem(place + d, heads), 0, keepdims=False)
            for d in range(heads)
        ]

    def deal(own):
        return [own[0]] + [lax.ppermute(own[d], "key", around(d)) for d in range(1, heads)]

    def gather(x):
        return [x] + [lax.ppermute(x, "key", across(d)) for d in range(1, ring)]

    def by_head(x):
        return jnp.transpose(x.astype(F32), (1, 0, 2))

    sds = jax.ShapeDtypeStruct
    lines = jnp.transpose(beta_raw_logits, (1, 0))[:, None, :]
    lines = jnp.pad(lines, ((0, 0), (0, 7), (0, 0)))
    pack = jnp.concatenate([by_head(key), by_head(raw_directions), lines], axis=1)
    packs = deal(chunks(pack))
    values = deal(chunks(by_head(value)))
    qs = deal(chunks(by_head(query).reshape(heads, rows, width)))

    km, wk, yz = call(
        functools.partial(block_kernel, heads, length, width),
        (
            sds((heads, width, length + width), F32),
            sds((heads, 2 * width, 2 * length), BF16),
            sds((heads, 3 * length, length + width), BF16),
        ),
        packs,
        scalars=scal,
        flops=heads * 20 * 6 * length**3,
        nbytes=heads * 10 * length * width * 4,
    )

    v_own = jnp.stack(values)

    v_pair = jnp.stack(gather(v_own))
    km_parts = gather(km)
    vb = call(
        functools.partial(value_kernel, heads, ring, length),
        sds((keys, width), BF16),
        [v_pair],
        scalars=scal,
        nbytes=keys * width * 6,
    )
    kmcat, packet = call(
        functools.partial(section_kernel, heads, ring, length),
        (
            sds((blocks, 3 * width, length + width), BF16),
            sds((width, blocks * length + width), F32),
        ),
        km_parts,
        scalars=scal,
        flops=blocks * 12 * length**3,
        nbytes=blocks * 8 * length * width * 4,
    )

    pair = [(s, s ^ 1) for s in range(sec_count)]
    rise = [(s, s + 1) for s in range(0, sec_count, 2)]
    v_far = [lax.ppermute(v_pair, "sec", rise)]
    k_far = [lax.ppermute(packet, "sec", rise)]
    for p in range(1, hops + 1):
        line = [(s, s + 2 * p) for s in range(sec_count - 2 * p)]
        v_got = jnp.stack(gather(lax.ppermute(v_own, "sec", line)))
        k_got = lax.ppermute(packet, "sec", line)
        v_far += [v_got, lax.ppermute(v_got, "sec", pair)]
        k_far += [k_got, lax.ppermute(k_got, "sec", pair)]

    def near(d):
        return call(
            functools.partial(near_kernel, d, heads, ring, length, width),
            (sds((rows, 3 * width), BF16), sds((rows, 128), F32), sds((rows, width), F32)),
            [qs[d], wk, yz, kmcat, vb],
            scratch=[pltpu.VMEM((rows, width), F32), pltpu.VMEM((rows, keys), F32)],
            scalars=scal,
            flops=blocks // 2 * rows * width * length * 14,
            nbytes=rows * width * 16,
            exps=blocks // 2 * rows * length,
        )

    order = [heads // 2] + [d for d in range(1, heads) if d != heads // 2] + [0]
    found = {d: near(d) for d in [0] + order[:-1]}
    far_count = 2 * hops + 1
    kc, vc = call(
        functools.partial(prep_kernel, hops, heads, ring, length),
        (sds((far_count, 3 * width, keys), BF16), sds((far_count, keys, width), BF16)),
        k_far + v_far,
        scratch=[pltpu.VMEM((width, keys + width), F32)],
        scalars=scal,
        flops=far_count * width * width * keys * 6,
        nbytes=far_count * keys * width * 16,
    )
    parts = 2

    def far(d):
        return call(
            functools.partial(far_kernel, parts),
            sds((rows, width), F32),
            list(found[d]) + [kc, vc],
            scratch=[
                pltpu.VMEM((parts, rows // parts, 1), F32),
                pltpu.VMEM((parts, rows // parts, 1), F32),
                pltpu.VMEM((parts, rows // parts, width), F32),
            ],
            scalars=scal,
            flops=rows * far_count * keys * width * 8,
            nbytes=rows * width * 20 + far_count * keys * width * 8,
            exps=rows * far_count * keys,
        )

    back = [None] * heads
    for d in order:
        piece = far(d)
        back[d] = lax.ppermute(piece, "key", around(-d)) if d else piece
    return call(
        functools.partial(join_kernel, heads, group),
        sds((length, q_count, width), BF16),
        back,
        scratch=[pltpu.VMEM((q_count, length, width), F32)],
        scalars=scal,
        nbytes=heads * rows * width * 6,
    )


def solution(mesh):
    rows = P(("sec", "key"), None, None)
    return jax.shard_map(
        steps,
        mesh=mesh,
        in_specs=(rows, rows, rows, rows, P(("sec", "key"), None)),
        out_specs=rows,
        check_vma=False,
    )
```

```python
import functools

import jax
import jax.numpy as jnp
from jax import lax
from jax.experimental import pallas as pl
from jax.experimental.pallas import tpu as pltpu
from jax.sharding import PartitionSpec as P


F32 = jnp.float32
BF16 = jnp.bfloat16
VMEM_LIMIT = 20 * 1024 * 1024
LOW = -1e30
LOG2_E = 1.4426950408889634


def halves(x):
    h = x.astype(BF16)
    return h, (x - h.astype(F32)).astype(BF16)


def left_cat(x):
    h, l = halves(x)
    return jnp.concatenate([h, l, h], axis=1)


def right_rows(x):
    h, l = halves(x)
    return jnp.concatenate([h, h, l], axis=0)


def mm(a, b):
    return lax.dot_general(a, b, (((1,), (0,)), ((), ())), preferred_element_type=F32)


def dot_nn(a, b):
    return mm(left_cat(a), right_rows(b))


def thirds(x):
    h = x.astype(BF16)
    rest = x - h.astype(F32)
    m = rest.astype(BF16)
    return h, m, (rest - m.astype(F32)).astype(BF16)


def dot_fine(a, b):
    ah, am, al = thirds(a)
    bh, bm, bl = thirds(b)
    return mm(
        jnp.concatenate([ah, am, al, ah, am, ah], axis=1),
        jnp.concatenate([bh, bh, bh, bm, bm, bl], axis=0),
    )


def call(kernel, out_shape, args, scratch=(), scalars=None, flops=0, nbytes=0, exps=0):
    vm = pl.BlockSpec(memory_space=pltpu.VMEM)
    sm = pl.BlockSpec(memory_space=pltpu.SMEM)
    specs = [vm] * len(args)
    if scalars is not None:
        specs = [sm] + specs
        args = [scalars] + list(args)
    outs = jax.tree.map(lambda _: vm, out_shape)
    return pl.pallas_call(
        kernel,
        out_shape=out_shape,
        in_specs=specs,
        out_specs=outs,
        scratch_shapes=list(scratch),
        compiler_params=pltpu.CompilerParams(vmem_limit_bytes=VMEM_LIMIT),
        cost_estimate=pl.CostEstimate(flops=flops, bytes_accessed=nbytes, transcendentals=exps),
    )(*args)


def ident(n):
    rows = lax.broadcasted_iota(jnp.int32, (n, n), 0)
    return (rows == lax.broadcasted_iota(jnp.int32, (n, n), 1)).astype(F32)


def block_kernel(heads, length, width, scal, *refs):
    packs = refs[:heads]
    km_ref, wk_ref, yz_ref = refs[heads:]
    place = scal[0]
    rows = lax.broadcasted_iota(jnp.int32, (length, length), 0)
    cols = lax.broadcasted_iota(jnp.int32, (length, length), 1)
    eye = ident(length)
    strict = rows > cols
    units, turned, betas, lows, xs = [], [], [], [], []
    for d in range(heads):
        w = packs[d][length : 2 * length]
        b_row = packs[d][2 * length : 2 * length + 1]
        beta = 2.0 / (1.0 + jnp.exp(-b_row))
        beta = jnp.transpose(jnp.broadcast_to(beta, (length, length)))
        unit = w / jnp.sqrt(jnp.sum(w * w, -1, keepdims=True) + 1e-06)
        across = jnp.transpose(unit)
        low = jnp.where(strict, beta * dot_fine(unit, across), 0.0)
        units.append(unit)
        turned.append(across)
        betas.append(beta)
        lows.append(low)
        level = (rows // 2 == cols // 2) & (rows % 2 == 1) & (cols % 2 == 0)
        xs.append(eye - jnp.where(level, low, 0.0))
    size = 2
    while size < length:
        step = min(4, length // size)
        level = (rows // (step * size) == cols // (step * size)) & (rows // size > cols // size)
        links = [dot_fine(xs[d], jnp.where(level, lows[d], 0.0)) for d in range(heads)]
        both = [
            dot_fine(links[d], jnp.concatenate([links[d], xs[d]], axis=1)) for d in range(heads)
        ]
        xs = [xs[d] - both[d][:, length:] for d in range(heads)]
        if step == 4:
            xs = [xs[d] + dot_fine(both[d][:, :length], xs[d]) for d in range(heads)]
        size *= step
    for d in range(heads):
        slot = lax.rem(place - d + heads, heads)
        unit, beta, across = units[d], betas[d], turned[d]
        kt = jnp.transpose(packs[d][0:length])
        kb = kt.astype(BF16)
        uh, ul = halves(unit)
        cross = mm(jnp.concatenate([uh, ul], axis=1), jnp.concatenate([kb, kb], axis=0))
        cross = jnp.where(strict, cross, 0.0)
        zy = dot_nn(xs[d], jnp.concatenate([beta * cross, beta[:, :width] * unit], axis=1))
        base = jnp.concatenate([kt, ident(width)], axis=1)
        km_ref[slot] = base - dot_nn(across, zy)
        ah, al = halves(across)
        wk_ref[slot] = jnp.concatenate(
            [
                jnp.concatenate([ah, kb], axis=1),
                jnp.concatenate([al, jnp.zeros_like(kb)], axis=1),
            ],
            axis=0,
        )
        yz_ref[slot] = right_rows(zy)


def section_kernel(heads, ring, length, scal, *refs):
    kms = refs[:ring]
    kmcat_ref, pack_ref = refs[ring:]
    low = scal[1]
    width = pack_ref.shape[0]
    blocks = heads * ring
    for r in range(ring):
        lane = lax.rem(low - r + ring, ring)
        for t in range(heads):
            kmcat_ref[t * ring + lane] = right_rows(kms[r][t])
    suffix = ident(width)
    for b in range(blocks - 1, -1, -1):
        got = mm(left_cat(suffix), kmcat_ref[b])
        pack_ref[:, b * length : (b + 1) * length] = got[:, :length]
        suffix = got[:, length:]
    pack_ref[:, blocks * length :] = suffix


def lay_values(heads, ring, length, scal, ref, store):
    for r in range(ring):
        lane = lax.rem(scal[1] - r + ring, ring)
        for d in range(heads):
            b = lax.rem(scal[0] - d + heads, heads) * ring + lane
            store(pl.ds(pl.multiple_of(b * length, length), length), ref[r, d].astype(BF16))


def value_kernel(heads, ring, length, scal, v_ref, vb_ref):
    def store(at, x):
        vb_ref[at] = x

    lay_values(heads, ring, length, scal, v_ref, store)


def near_kernel(d, heads, ring, length, width, scal, q_ref, *refs):
    wk_ref, yz_ref, kmcat_ref, vb_ref, qcat_ref, ml_ref, acc_ref, q_s, s_s = refs
    place, low = scal[0], scal[1]
    rows = q_ref.shape[0]
    scale = width ** (-0.5) * LOG2_E
    blocks = heads * ring
    keys = blocks * length
    token = lax.rem(lax.broadcasted_iota(jnp.int32, (rows, length), 0), length)
    causal = token >= lax.broadcasted_iota(jnp.int32, (rows, length), 1)
    lane_id = lax.broadcasted_iota(jnp.int32, (rows // 2, 128), 1)

    def at(b):
        return pl.ds(pl.multiple_of(b * length, length), length)

    t = lax.rem(place - d + heads, heads)
    b_own = t * ring + low
    qf = q_ref[...]
    q = qf.astype(BF16)
    both = mm(jnp.concatenate([q, q], axis=1), wk_ref[t])
    qw = jnp.where(causal, both[:, :length], 0.0)
    u = mm(left_cat(qw), yz_ref[t])
    q_s[...] = (qf - u[:, length:]) * scale
    s_s[:, at(b_own)] = jnp.where(causal, (both[:, length:] - u[:, :length]) * scale, LOW)

    def clear(b, c):
        s_s[:, at(b)] = jnp.full((rows, length), LOW, F32)
        return c

    lax.fori_loop(b_own + 1, blocks, clear, 0)

    def step(i, c):
        b = b_own - 1 - i
        both = mm(left_cat(q_s[...]), kmcat_ref[b])
        s_s[:, at(b)] = both[:, :length]
        q_s[...] = both[:, length:]
        return c

    lax.fori_loop(0, b_own, step, 0)
    qcat_ref[...] = left_cat(q_s[...])

    def finish(n):
        for half in range(2):
            part = slice(half * rows // 2, (half + 1) * rows // 2)
            s = s_s[part, :n]
            top = jnp.max(s, -1, keepdims=True)
            p = jnp.exp2(s - top)
            ml_ref[part] = jnp.where(lane_id < 64, top, jnp.sum(p, -1, keepdims=True))
            acc_ref[part] = mm(p.astype(BF16), vb_ref[:n])

    small = b_own < blocks // 2

    @pl.when(small)
    def _():
        finish(keys // 2)

    @pl.when(jnp.logical_not(small))
    def _():
        finish(keys)


def prep_kernel(hops, heads, ring, length, scal, *refs):
    n = 2 * hops + 1
    packs, values = refs[:n], refs[n : 2 * n]
    kc_ref, vc_ref, got = refs[2 * n :]
    sec = scal[2]
    core = lax.rem(sec, 2)
    width = got.shape[0]
    keys = got.shape[1] - width
    got_map = ident(width)

    def take(dst, i):
        dst[...] = packs[i][...]

    def take_v(dist, i):
        def store(at, x):
            vc_ref[dist - 1, at] = x

        lay_values(heads, ring, length, scal, values[i], store)

    for dist in range(1, n + 1):
        p = dist // 2
        if dist % 2 == 0:
            take(got, 2 * p - 1)
            take_v(dist, 2 * p - 1)
        else:

            @pl.when(core == 1)
            def _():
                take(got, 2 * p)
                take_v(dist, 2 * p)

            if p + 1 <= hops:

                @pl.when(core == 0)
                def _():
                    take(got, 2 * p + 2)
                    take_v(dist, 2 * p + 2)

        moved = mm(left_cat(got_map), right_rows(got[...])) if dist > 1 else got[...]
        kc_ref[dist - 1] = right_rows(moved[:, :keys])
        got_map = moved[:, keys:]


def far_kernel(parts, scal, q_ref, ml_ref, acc_ref, k_ref, v_ref, out_ref, m_s, l_s, a_s):
    size = q_ref.shape[0] // parts
    spots = [slice(p * size, (p + 1) * size) for p in range(parts)]
    for i, part in enumerate(spots):
        m_s[i] = ml_ref[part, 0:1]
        l_s[i] = ml_ref[part, 64:65]
        a_s[i] = acc_ref[part]

    def step(sec, c):
        s = mm(q_ref[spots[0]], k_ref[sec])
        for i in range(parts):
            coming = mm(q_ref[spots[i + 1]], k_ref[sec]) if i + 1 < parts else None
            old = m_s[i]
            top = jnp.maximum(old, jnp.max(s, -1, keepdims=True))
            p = jnp.exp2(s - top)
            f = jnp.exp2(old - top)
            m_s[i] = top
            l_s[i] = l_s[i] * f + jnp.sum(p, -1, keepdims=True)
            a_s[i] = a_s[i] * f + mm(p.astype(BF16), v_ref[sec])
            s = coming
        return c

    lax.fori_loop(0, jnp.minimum(scal[2], k_ref.shape[0]), step, 0)
    for i, part in enumerate(spots):
        out_ref[part] = a_s[i] / l_s[i]


def join_kernel(heads, group, scal, *refs):
    out_ref, held = refs[heads:]
    length = out_ref.shape[0]
    for d in range(heads):
        at = lax.rem(scal[0] + d, heads)
        for g in range(group):
            held[at * group + g] = refs[d][g * length : (g + 1) * length]
    out_ref[...] = jnp.swapaxes(held[...], 0, 1).astype(BF16)


def steps(query, key, value, raw_directions, beta_raw_logits):
    length, q_count, width = query.shape
    heads = key.shape[1]
    group = q_count // heads
    key_count, sec_count = lax.axis_size("key"), lax.axis_size("sec")
    ring = key_count // heads
    hops = sec_count // 2 - 1
    key_index, sec_index = lax.axis_index("key"), lax.axis_index("sec")
    place, low = key_index // ring, key_index % ring
    scal = jnp.stack([place, low, sec_index]).astype(jnp.int32)
    blocks = heads * ring
    rows = group * length
    keys = blocks * length

    def around(d):
        return [(k, ((k // ring + d) % heads) * ring + k % ring) for k in range(key_count)]

    def across(d):
        return [(k, (k // ring) * ring + (k % ring + d) % ring) for k in range(key_count)]

    def chunks(x):
        return [
            lax.dynamic_index_in_dim(x, lax.rem(place + d, heads), 0, keepdims=False)
            for d in range(heads)
        ]

    def deal(own):
        return [own[0]] + [lax.ppermute(own[d], "key", around(d)) for d in range(1, heads)]

    def gather(x):
        return [x] + [lax.ppermute(x, "key", across(d)) for d in range(1, ring)]

    def by_head(x):
        return jnp.transpose(x.astype(F32), (1, 0, 2))

    sds = jax.ShapeDtypeStruct
    lines = jnp.transpose(beta_raw_logits, (1, 0))[:, None, :]
    lines = jnp.pad(lines, ((0, 0), (0, 7), (0, 0)))
    pack = jnp.concatenate([by_head(key), by_head(raw_directions), lines], axis=1)
    packs = deal(chunks(pack))
    values = deal(chunks(by_head(value)))
    qs = deal(chunks(by_head(query).reshape(heads, rows, width)))

    km, wk, yz = call(
        functools.partial(block_kernel, heads, length, width),
        (
            sds((heads, width, length + width), F32),
            sds((heads, 2 * width, 2 * length), BF16),
            sds((heads, 3 * length, length + width), BF16),
        ),
        packs,
        scalars=scal,
        flops=heads * 20 * 6 * length**3,
        nbytes=heads * 10 * length * width * 4,
    )

    v_own = jnp.stack(values)

    v_pair = jnp.stack(gather(v_own))
    km_parts = gather(km)
    vb = call(
        functools.partial(value_kernel, heads, ring, length),
        sds((keys, width), BF16),
        [v_pair],
        scalars=scal,
        nbytes=keys * width * 6,
    )
    kmcat, packet = call(
        functools.partial(section_kernel, heads, ring, length),
        (
            sds((blocks, 3 * width, length + width), BF16),
            sds((width, blocks * length + width), F32),
        ),
        km_parts,
        scalars=scal,
        flops=blocks * 12 * length**3,
        nbytes=blocks * 8 * length * width * 4,
    )

    pair = [(s, s ^ 1) for s in range(sec_count)]
    rise = [(s, s + 1) for s in range(0, sec_count, 2)]
    v_far = [lax.ppermute(v_pair, "sec", rise)]
    k_far = [lax.ppermute(packet, "sec", rise)]
    for p in range(1, hops + 1):
        line = [(s, s + 2 * p) for s in range(sec_count - 2 * p)]
        v_got = jnp.stack(gather(lax.ppermute(v_own, "sec", line)))
        k_got = lax.ppermute(packet, "sec", line)
        v_far += [v_got, lax.ppermute(v_got, "sec", pair)]
        k_far += [k_got, lax.ppermute(k_got, "sec", pair)]

    def near(d):
        return call(
            functools.partial(near_kernel, d, heads, ring, length, width),
            (sds((rows, 3 * width), BF16), sds((rows, 128), F32), sds((rows, width), F32)),
            [qs[d], wk, yz, kmcat, vb],
            scratch=[pltpu.VMEM((rows, width), F32), pltpu.VMEM((rows, keys), F32)],
            scalars=scal,
            flops=blocks // 2 * rows * width * length * 14,
            nbytes=rows * width * 16,
            exps=blocks // 2 * rows * length,
        )

    order = [heads // 2] + [d for d in range(1, heads) if d != heads // 2] + [0]
    found = {d: near(d) for d in [0] + order[:-1]}
    far_count = 2 * hops + 1
    kc, vc = call(
        functools.partial(prep_kernel, hops, heads, ring, length),
        (sds((far_count, 3 * width, keys), BF16), sds((far_count, keys, width), BF16)),
        k_far + v_far,
        scratch=[pltpu.VMEM((width, keys + width), F32)],
        scalars=scal,
        flops=far_count * width * width * keys * 6,
        nbytes=far_count * keys * width * 16,
    )
    parts = 2

    def far(d):
        return call(
            functools.partial(far_kernel, parts),
            sds((rows, width), F32),
            list(found[d]) + [kc, vc],
            scratch=[
                pltpu.VMEM((parts, rows // parts, 1), F32),
                pltpu.VMEM((parts, rows // parts, 1), F32),
                pltpu.VMEM((parts, rows // parts, width), F32),
            ],
            scalars=scal,
            flops=rows * far_count * keys * width * 8,
            nbytes=rows * width * 20 + far_count * keys * width * 8,
            exps=rows * far_count * keys,
        )

    back = [None] * heads
    for d in order:
        piece = far(d)
        back[d] = lax.ppermute(piece, "key", around(-d)) if d else piece
    return call(
        functools.partial(join_kernel, heads, group),
        sds((length, q_count, width), BF16),
        back,
        scratch=[pltpu.VMEM((q_count, length, width), F32)],
        scalars=scal,
        nbytes=heads * rows * width * 6,
    )


def solution(mesh):
    rows = P(("sec", "key"), None, None)
    return jax.shard_map(
        steps,
        mesh=mesh,
        in_specs=(rows, rows, rows, rows, P(("sec", "key"), None)),
        out_specs=rows,
        check_vma=False,
    )
```
